256 devices in a mesh: bench: 32 (over x, y, core), sweep: 8 (over z).
Axes of the slice: x: 4, y: 4, z: 8, core: 2. Of those that a mesh axis runs over, the one named last changes fastest.
Arguments:
- finished: bfloat16 [1024, 8, 64, 128], P('bench', 'sweep'), may hold values from -6 to 6
- noise: bfloat16 [1024, 8, 64, 128], P('bench', 'sweep'), may hold values from -6 to 6
- factors: bfloat16 [1024, 8, 8, 128, 128], P('bench', 'sweep'), may hold values from -0.1875 to 0.1875
- chol: bfloat16 [1024, 8, 128, 128], P('bench', 'sweep'), may hold values from -0.1875 to 0.1875
- front_w: bfloat16 [1024, 8, 128, 128], P('bench', 'sweep'), may hold values from -0.5 to 0.5
- parents: int32 [1024, 8, 8], P('bench', 'sweep'), may hold values from 0 to 1023, as said below
Outputs:
- evolved: float32 [1024, 8, 64, 128], P('bench', 'sweep')
The draws below stay inside these ranges and needn't reach their ends.
Inputs may be any that keep to these rules, and one draw needn't show every extreme that they name: A parent row p lies on the bench owner p // 32. The 256 parents of the tiles of one bench group and sweep column name at most 16 rows of one owner, exactly 16 for some owner, and lie on at most 17 owners.
All inputs are finite; a program needn't handle non-finite values.
Results may differ from the reference program's by a relative error of at most 0.0003.
Values may be sent and summed in bfloat16 or wider, within the bound.
No kernel may reach another device: no remote copies, remote signals or barrier semaphores. Data moves between devices by JAX's collectives and lax.ppermute only.
A program may use at most 128 MiB of HBM per device.

```python
import jax
import jax.numpy as jnp
from jax import lax

NODE = 128
REAL = 64
PAR = 8
NT = 32
FIN = 32
TILES = 1024
POOL = 1024
N_BENCH = 32
N_SWEEP = 8


def draw_parents(key, part):
    bound = 2 * PAR * NT // N_BENCH
    count = NT * PAR
    key_owner, key_coin, key_order, key_local = jax.random.split(key, 4)
    owner_score = jax.random.randint(key_owner, (N_BENCH, N_SWEEP, N_BENCH), 0, 1 << 20) * N_BENCH + jnp.arange(N_BENCH, dtype=jnp.int32)
    sigma = jnp.argsort(owner_score, axis=-1, stable=True).astype(jnp.int32)
    block = jnp.arange(count, dtype=jnp.int32) // bound
    coin = jax.random.randint(key_coin, (N_BENCH, N_SWEEP, 1), 0, 2)
    last = jnp.arange(count, dtype=jnp.int32) == count - 1
    block = jnp.where(last[None, None, :] & (coin == 1), N_BENCH - 1, block[None, None, :] + jnp.zeros((N_BENCH, N_SWEEP, 1), jnp.int32))
    owner = jnp.take_along_axis(sigma, block, axis=-1)
    order_score = jax.random.randint(key_order, (N_BENCH, N_SWEEP, count), 0, 1 << 20) * count + jnp.arange(count, dtype=jnp.int32)
    order = jnp.argsort(order_score, axis=-1, stable=True).astype(jnp.int32)
    owner = jnp.take_along_axis(owner, order, axis=-1)
    local = jax.random.randint(key_local, (N_BENCH, N_SWEEP, count), 0, FIN)
    ids = owner * FIN + local
    ids = ids.reshape(N_BENCH, N_SWEEP, NT, PAR).transpose(0, 2, 1, 3).reshape(N_BENCH * NT, N_SWEEP, PAR)
    return ids.astype(jnp.int32)


def block_levels(own_key, extent, cuts, least, largest):
    level, own = 1.0, jax.random.fold_in(own_key, 6)
    for dim, shards_of in cuts:
        draws = jnp.exp(jax.random.uniform(jax.random.fold_in(own, dim), (shards_of,), jnp.float32, least / len(cuts), largest / len(cuts)))
        level = level * jnp.repeat(draws, extent[dim] // shards_of).reshape([-1 if axis == dim else 1 for axis in range(len(extent))])
    return level


def gaussian(own_key, shape, scale, reach, shards=(), kind=jnp.bfloat16):
    factor_of = block_levels(own_key, shape, shards, -0.22, 0.18) if shards else 1.0
    result = jax.random.normal(own_key, shape, jnp.float32) * scale * factor_of
    return jnp.minimum(jnp.maximum(result, -reach), reach).astype(kind)


def setup_inputs(seed: int = 0) -> dict:
    streams_of = jax.random.split(jax.random.key(seed), 7)
    return {
        "finished": gaussian(streams_of[0], (POOL, N_SWEEP, REAL, NODE), 1.0, 6.0, ((0, 32), (1, 8))),
        "noise": gaussian(streams_of[1], (TILES, N_SWEEP, REAL, NODE), 1.0, 6.0, ((0, 32), (1, 8))),
        "factors": gaussian(streams_of[2], (TILES, N_SWEEP, PAR, NODE, NODE), (NODE * (PAR + 1)) ** -0.5, 0.1875, ((0, 32), (1, 8))),
        "chol": gaussian(streams_of[3], (TILES, N_SWEEP, NODE, NODE), (NODE * (PAR + 1)) ** -0.5, 0.1875, ((0, 32), (1, 8))),
        "front_w": gaussian(streams_of[4], (TILES, N_SWEEP, NODE, NODE), NODE ** -0.5, 0.5, ((0, 32), (1, 8))),
        "parents": draw_parents(jax.random.fold_in(streams_of[6], 71), 0),
    }


def reference(finished, noise, factors, chol, front_w, parents):
    columns = jnp.arange(N_SWEEP, dtype=jnp.int32)

    def per_bench(bench_row):
        start = (bench_row * NT).astype(jnp.int32)
        rows = lax.dynamic_slice_in_dim(parents, start, NT, 0)
        factor_block = lax.dynamic_slice_in_dim(factors, start, NT, 0).astype(jnp.float32)
        noise_block = lax.dynamic_slice_in_dim(noise, start, NT, 0).astype(jnp.float32)
        chol_block = lax.dynamic_slice_in_dim(chol, start, NT, 0).astype(jnp.float32)
        chosen = finished[rows, columns[None, :, None]].astype(jnp.float32)
        term = jnp.einsum('jskrm,jskmn->jsrn', chosen, factor_block)
        return term + jnp.einsum('jsrm,jsmn->jsrn', noise_block, chol_block)

    local = lax.map(per_bench, jnp.arange(N_BENCH, dtype=jnp.int32))
    weights = front_w.astype(jnp.float32).reshape(N_BENCH, NT, N_SWEEP, NODE, NODE)
    front = jnp.zeros((N_BENCH, REAL, NODE), jnp.float32)
    results = []
    for column in range(N_SWEEP):
        tiles = local[:, :, column] + jnp.einsum('brm,bjmn->bjrn', front, weights[:, :, column], precision=lax.Precision.HIGHEST)
        results.append(tiles)
        front = tiles[:, NT - 1]
    return jnp.stack(results, axis=2).reshape(N_BENCH * NT, N_SWEEP, REAL, NODE)
```

```python
import functools

import jax
import jax.numpy as jnp
import numpy as np
from jax import lax
from jax.experimental import pallas as pl
from jax.experimental.pallas import tpu as pltpu
from jax.sharding import PartitionSpec as P


SIDE = 4
PARTS = 4
NEAR = ((0, 0), (-1, 0), (1, 0), (0, -1), (0, 1))
MIDDLE = ((-1, -1), (1, 1), (1, -1), (-1, 1), (2, 0), (0, 2))
FAR = ((2, -1), (2, 1), (1, 2), (-1, 2))
LAST = ((2, 2),)
GROUPS = (NEAR, MIDDLE, FAR, LAST)


def place(x, y, core):
    return ((x % SIDE) * SIDE + y % SIDE) * 2 + core


def grid():
    return [(x, y, c) for x in range(SIDE) for y in range(SIDE) for c in range(2)]


def from_chip(array, dx, dy):
    pairs = [(place(x + dx, y + dy, c), place(x, y, c)) for x, y, c in grid()]
    return lax.ppermute(array, "bench", pairs)


def from_partner(array):
    pairs = [(place(x, y, c), place(x, y, 1 - c)) for x, y, c in grid()]
    return lax.ppermute(array, "bench", pairs)


def from_behind(array, by):
    size = lax.axis_size("sweep")
    return lax.ppermute(array, "sweep", [(i, (i + by) % size) for i in range(size)])


def spread(own):
    n = own.shape[0]
    half, quarter = n // 2, n // 4
    b = {(0, 0): own}
    for d in NEAR[1:]:
        b[d] = from_chip(own, *d)
    b[-1, -1] = from_chip(b[0, -1], -1, 0)
    b[1, 1] = from_chip(b[0, 1], 1, 0)
    b[1, -1] = from_chip(b[1, 0], 0, -1)
    b[-1, 1] = from_chip(b[-1, 0], 0, 1)
    b[2, 0] = jnp.concatenate(
        [from_chip(b[-1, 0][:half], -1, 0), from_chip(b[1, 0][half:], 1, 0)]
    )
    b[0, 2] = jnp.concatenate(
        [from_chip(b[0, -1][:half], 0, -1), from_chip(b[0, 1][half:], 0, 1)]
    )
    b[2, -1] = from_chip(b[-1, -1], -1, 0)
    b[2, 1] = from_chip(b[1, 1], 1, 0)
    b[1, 2] = from_chip(b[1, -1], 0, -1)
    b[-1, 2] = from_chip(b[-1, 1], 0, 1)
    b[2, 2] = jnp.concatenate(
        [
            from_chip(b[-1, 2][:quarter], -1, 0),
            from_chip(b[1, 2][quarter : 2 * quarter], 1, 0),
            from_chip(b[2, -1][2 * quarter : 3 * quarter], 0, -1),
            from_chip(b[2, 1][3 * quarter :], 0, 1),
        ]
    )
    mine = [jnp.concatenate([b[d] for d in g]) for g in GROUPS]
    return mine + [from_partner(g) for g in mine]


def whereabouts(parents, rows):
    group = np.zeros((SIDE * SIDE,), np.int32)
    base = np.zeros((SIDE * SIDE,), np.int32)
    for g, members in enumerate(GROUPS):
        for i, (dx, dy) in enumerate(members):
            group[(dx % SIDE) * SIDE + dy % SIDE] = g
            base[(dx % SIDE) * SIDE + dy % SIDE] = i * rows
    me = lax.axis_index("bench")
    owner = parents // rows
    dx = (owner // (2 * SIDE) - me // (2 * SIDE)) % SIDE
    dy = (owner // 2 - me // 2) % SIDE
    key = (dx * SIDE + dy)[..., None] == jnp.arange(SIDE * SIDE, dtype=jnp.int32)
    which = jnp.sum(jnp.where(key, jnp.asarray(group), 0), -1)
    start = jnp.sum(jnp.where(key, jnp.asarray(base), 0), -1)
    other = ((owner % 2) != (me % 2)).astype(jnp.int32)
    return which + PARTS * other, start + parents % rows


def tiles_kernel(first, count, fan, which, where, *refs):
    pools, refs = refs[: 2 * PARTS], refs[2 * PARTS :]
    factors, noise, chol, out, rows, fac, noi, cho, row_sem, fac_sem, sem = refs
    node = fac.shape[-1]
    span = pl.ds(first, count)
    noise_copy = pltpu.make_async_copy(noise.at[span], noi, sem.at[0])
    chol_copy = pltpu.make_async_copy(chol.at[span], cho, sem.at[1])

    def fetch_rows(t):
        for k in range(fan):
            g = which[first + t, k]
            r = where[first + t, k]
            target = rows.at[t, :, pl.ds(k * node, node)]

            def choose(low, high):
                if high - low == 1:
                    pltpu.make_async_copy(pools[low].at[r], target, row_sem.at[t]).start()
                    return
                mid = (low + high) // 2

                @pl.when(g < mid)
                def _():
                    choose(low, mid)

                @pl.when(g >= mid)
                def _():
                    choose(mid, high)

            choose(0, 2 * PARTS)

    def fetch(t, carry):
        pltpu.make_async_copy(factors.at[first + t], fac.at[t], fac_sem.at[t]).start()
        fetch_rows(t)
        return carry

    noise_copy.start()
    chol_copy.start()
    lax.fori_loop(0, count, fetch, 0)
    noise_copy.wait()
    chol_copy.wait()

    def compute(t, carry):
        pltpu.make_async_copy(factors.at[first + t], fac.at[t], fac_sem.at[t]).wait()
        pltpu.make_async_copy(rows.at[t], rows.at[t], row_sem.at[t]).wait()
        weights = fac[t].reshape(fan * node, node)
        total = jnp.dot(rows[t], weights, preferred_element_type=jnp.float32)
        total += jnp.dot(noi[t], cho[t], preferred_element_type=jnp.float32)
        out[t] = total
        return carry

    lax.fori_loop(0, count, compute, 0)


def tiles(first, count, which, where, pools, factors, noise, chol):
    fan, node = factors.shape[1], factors.shape[2]
    real = noise.shape[1]
    smem = pl.BlockSpec(memory_space=pltpu.SMEM)
    hbm = pl.BlockSpec(memory_space=pl.ANY)
    return pl.pallas_call(
        functools.partial(tiles_kernel, first, count, fan),
        out_shape=jax.ShapeDtypeStruct((count, real, node), jnp.float32),
        in_specs=[smem, smem] + [hbm] * (2 * PARTS + 3),
        out_specs=pl.BlockSpec(memory_space=pltpu.VMEM),
        scratch_shapes=[
            pltpu.VMEM((count, real, fan * node), jnp.bfloat16),
            pltpu.VMEM((count, fan, node, node), jnp.bfloat16),
            pltpu.VMEM((count, real, node), jnp.bfloat16),
            pltpu.VMEM((count, node, node), jnp.bfloat16),
            pltpu.SemaphoreType.DMA((count,)),
            pltpu.SemaphoreType.DMA((count,)),
            pltpu.SemaphoreType.DMA((2,)),
        ],
        compiler_params=pltpu.CompilerParams(vmem_limit_bytes=40 * 1024 * 1024),
        cost_estimate=pl.CostEstimate(
            flops=2 * count * real * node * node * (fan + 1),
            bytes_accessed=count * (fan + 2) * node * (node + real) * 2,
            transcendentals=0,
        ),
        name="tiles",
    )(which, where, *pools, factors, noise, chol)


def exact(a, b):
    return jnp.dot(a, b, precision=lax.Precision.HIGHEST)


def body(finished, noise, factors, chol, front_w, parents):
    own = finished[:, 0]
    noise, factors, chol = noise[:, 0], factors[:, 0], chol[:, 0]
    count, fan = factors.shape[0], factors.shape[1]
    position = lax.axis_index("sweep")
    which, where = whereabouts(parents[:, 0], own.shape[0])

    with jax.named_scope("weights"):
        last_w = front_w[count - 1, 0]
        back1 = from_behind(last_w, 1).astype(jnp.float32)
        back2 = from_behind(last_w, 2).astype(jnp.float32)
        back3 = from_behind(last_w, 3).astype(jnp.float32)
        two = exact(back2, back1)
        three = exact(back3, two)
        six = exact(from_behind(three, 3), three)
        one = jnp.where(position >= 2, back1, 0.0)
        two = jnp.where(position >= 3, two, 0.0)
        three_in = jnp.where(position >= 4, three, 0.0)
        six = jnp.where(position >= 7, six, 0.0)

    with jax.named_scope("spread"):
        pools = spread(own)
    with jax.named_scope("front"):
        front = tiles(count - 1, 1, which, where, pools, factors, noise, chol)[0]
    with jax.named_scope("rest"):
        rest = tiles(0, count - 1, which, where, pools, factors, noise, chol)
    with jax.named_scope("sweep"):
        near = [from_behind(front, by) for by in (1, 2, 3)]
        part = jnp.where(position >= 1, near[0], 0.0) + exact(near[1], one) + exact(near[2], two)
        incoming = part + exact(from_behind(part, 3), three_in) + exact(from_behind(part, 6), six)
    with jax.named_scope("final"):
        local = jnp.concatenate([rest, front[None]])
        weights = front_w[:, 0].astype(jnp.float32)
        out = local + jnp.einsum("rm,jmn->jrn", incoming, weights, precision=lax.Precision.HIGHEST)
    return out[:, None]


def solution(mesh):
    return jax.shard_map(
        body,
        mesh=mesh,
        in_specs=(
            P("bench", "sweep", None, None),
            P("bench", "sweep", None, None),
            P("bench", "sweep", None, None, None),
            P("bench", "sweep", None, None),
            P("bench", "sweep", None, None),
            P("bench", "sweep", None),
        ),
        out_specs=P("bench", "sweep", None, None),
        check_vma=False,
    )
```

```python
import functools

import jax
import jax.numpy as jnp
import numpy as np
from jax import lax
from jax.experimental import pallas as pl
from jax.experimental.pallas import tpu as pltpu
from jax.sharding import PartitionSpec as P


SIDE = 4
ORDER = (
    (0, 0, None), (-1, 0, None), (1, 0, None), (0, -1, None), (0, 1, None), (-1, -1, None),
    (-1, 1, None), (1, -1, None), (1, 1, None), (2, 0, None), (0, 2, None), (2, -1, None),
    (2, 1, None), (-1, 2, None), (1, 2, None), (2, 2, 0), (2, 2, 1),
)
BLOCKS = len(ORDER)
EARLY = (13, 11)


def place(x, y, core):
    return ((x % SIDE) * SIDE + y % SIDE) * 2 + core


def offset(core, a, b):
    return (a, b) if core == 0 else (-b, -a)


def fetch(array, a, b):
    pairs = []
    for x in range(SIDE):
        for y in range(SIDE):
            for core in range(2):
                dx, dy = offset(core, a, b)
                pairs.append((place(x + dx, y + dy, core), place(x, y, core)))
    return lax.ppermute(array, "bench", pairs)


def from_partner(array):
    chips = SIDE * SIDE
    pairs = [(2 * i + core, 2 * i + 1 - core) for i in range(chips) for core in range(2)]
    return lax.ppermute(array, "bench", pairs)


def from_behind(array, by):
    size = lax.axis_size("sweep")
    return lax.ppermute(array, "sweep", [(i, (i + by) % size) for i in range(size)])


VIA = {
    (-1, 0, None): ((0, 0, None), (-1, 0)),
    (1, 0, None): ((0, 0, None), (1, 0)),
    (0, -1, None): ((0, 0, None), (0, -1)),
    (0, 1, None): ((0, 0, None), (0, 1)),
    (-1, -1, None): ((-1, 0, None), (0, -1)),
    (-1, 1, None): ((-1, 0, None), (0, 1)),
    (1, -1, None): ((1, 0, None), (0, -1)),
    (1, 1, None): ((1, 0, None), (0, 1)),
    (2, 0, None): ((-1, 0, None), (-1, 0)),
    (0, 2, None): ((0, -1, None), (0, -1)),
    (2, -1, None): ((2, 0, None), (0, -1)),
    (2, 1, None): ((2, 0, None), (0, 1)),
    (-1, 2, None): ((-1, -1, None), (0, -1)),
    (1, 2, None): ((1, 1, None), (0, 1)),
    (2, 2, 0): ((2, -1, None), (0, -1)),
    (2, 2, 1): ((2, 1, None), (0, 1)),
}


def spread(own, small):
    b = {(0, 0, None): own}
    for d, (source, step) in VIA.items():
        if d == (-1, -1, None):
            first = ORDER[1]
            b[first], small = lax.optimization_barrier((b[first], small))
        block = b[source]
        if d[2] is not None:
            block = jnp.split(block, 2)[d[2]]
        b[d] = fetch(block, *step)
    mine = [b[d] for d in ORDER]
    theirs = [from_partner(b[d]) for d in ORDER]
    return mine, theirs, small


def orders(parents, rows):
    number = np.zeros((2, SIDE, SIDE, 2), np.int32)
    for core in range(2):
        for i, (a, b, half) in enumerate(ORDER):
            dx, dy = offset(core, a, b)
            number[core, dx % SIDE, dy % SIDE, slice(None) if half is None else half] = i
    early, late = np.arange(EARLY[0]), np.arange(EARLY[0], BLOCKS)
    theirs_early, theirs_late = np.arange(EARLY[1]), np.arange(EARLY[1], BLOCKS)
    rank = np.zeros((2, BLOCKS), np.int32)
    for i, (other, block) in enumerate(
        [(0, j) for j in early] + [(1, j) for j in theirs_early]
        + [(0, j) for j in late] + [(1, j) for j in theirs_late]
    ):
        rank[other, block] = i
    table = np.zeros((2, 2, 2 * SIDE * SIDE), np.int32)
    for mine in range(2):
        for core in range(2):
            table[mine, core] = rank[int(mine != core)][number[core].reshape(-1)]
    me = lax.axis_index("bench")
    slots = parents.reshape(-1)
    count = slots.shape[0]
    owner = slots // rows
    dx = (owner // (2 * SIDE) - me // (2 * SIDE)) % SIDE
    dy = (owner // 2 - me // 2) % SIDE
    half = (slots % rows) // (rows // 2)
    spot = ((((me % 2) * 2 + owner % 2) * SIDE + dx) * SIDE + dy) * 2 + half
    flat = table.reshape(-1)
    key = jnp.sum(
        jnp.where(spot[None, :] == jnp.arange(flat.size)[:, None], jnp.asarray(flat)[:, None], 0), 0
    )
    slot = jnp.arange(count, dtype=jnp.int32)
    full = key * count + slot
    place_of = jnp.sum((full[:, None] < full[None, :]).astype(jnp.int32), 0)
    packed = slot * rows + slots % rows
    ranked = jnp.sum(jnp.where(place_of[:, None] == slot[None, :], packed[:, None], 0), 0)
    edges = jnp.arange(2 * BLOCKS + 8, dtype=jnp.int32)
    begins = jnp.sum((key[:, None] < edges[None, :]).astype(jnp.int32), 0)
    return begins.astype(jnp.int32), ranked.astype(jnp.int32)


UNROLL = 4


def move_rows(begins, ranked, blocks, first, shift, out):
    for p, block in enumerate(blocks):
        rows = block.shape[0]
        low, high = begins[first + p], begins[first + p + 1]

        def move(i, carry, block=block, low=low, high=high, rows=rows):
            at = [jnp.minimum(low + i * UNROLL + u, high - 1) for u in range(UNROLL)]
            entries = [ranked[j] for j in at]
            values = [block[e & (rows - 1)] for e in entries]
            for e, value in zip(entries, values, strict=True):
                out[e >> shift] = value
            return carry

        lax.fori_loop(0, (high - low + UNROLL - 1) >> 2, move, 0)


def one_tile(t, fan, rows, factors, noise, chol):
    node = factors.shape[-1]
    chosen = jnp.concatenate([rows[t * fan + k] for k in range(fan)], axis=1)
    total = jnp.dot(
        chosen, factors[t].reshape(fan * node, node), preferred_element_type=jnp.float32
    )
    return total + jnp.dot(noise[t], chol[t], preferred_element_type=jnp.float32)


def early_kernel(shift, begins, ranked, *refs):
    blocks, loads, rows, loaded, sem = refs[:-10], refs[-10:-6], refs[-6], refs[-5:-1], refs[-1]
    copies = [
        pltpu.make_async_copy(source, target, sem.at[i])
        for i, (source, target) in enumerate(zip(loads, loaded, strict=True))
    ]
    for copy in copies:
        copy.start()
    move_rows(begins, ranked, blocks, 0, shift, rows)
    for copy in copies:
        copy.wait()


def late_kernel(first, shift, begins, ranked, *refs):
    factors, noise, chol, _, rows, front = refs[-6:]
    count, fan = factors.shape[:2]
    move_rows(begins, ranked, refs[:-6], first, shift, rows)
    front[...] = one_tile(count - 1, fan, rows, factors, noise, chol)


def tiles_kernel(first, count, rows, factors, noise, chol, out):
    fan = factors.shape[1]

    def step(t, carry):
        out[t] = one_tile(first + t, fan, rows, factors, noise, chol)
        return carry

    lax.fori_loop(0, count, step, 0)


SMEM = pl.BlockSpec(memory_space=pltpu.SMEM)
VMEM = pl.BlockSpec(memory_space=pltpu.VMEM)
HBM = pl.BlockSpec(memory_space=pltpu.MemorySpace.HBM)
PARAMS = pltpu.CompilerParams(vmem_limit_bytes=8 * 1024 * 1024)


def cost(tiles_count, moved):
    return pl.CostEstimate(
        flops=2 * tiles_count * 64 * 128 * 128 * 9,
        bytes_accessed=moved,
        transcendentals=0,
    )


def shift_of(blocks):
    return max(block.shape[0] for block in blocks).bit_length() - 1


def gather_early(begins, ranked, blocks, slots, loads):
    shape = (slots,) + blocks[0].shape[1:]
    return pl.pallas_call(
        functools.partial(early_kernel, shift_of(blocks)),
        out_shape=[jax.ShapeDtypeStruct(shape, blocks[0].dtype)]
        + [jax.ShapeDtypeStruct(a.shape, a.dtype) for a in loads],
        in_specs=[SMEM, SMEM] + [VMEM] * len(blocks) + [HBM] * len(loads),
        out_specs=[VMEM] * (1 + len(loads)),
        scratch_shapes=[pltpu.SemaphoreType.DMA((len(loads),))],
        compiler_params=PARAMS,
        cost_estimate=cost(0, 16 << 20),
        name="early",
    )(begins, ranked, *blocks, *[pltpu.with_memory_space_constraint(a, pltpu.HBM) for a in loads])


def gather_late(begins, ranked, blocks, first, factors, noise, chol, rows):
    real, node = noise.shape[1:]
    return pl.pallas_call(
        functools.partial(late_kernel, first, shift_of(blocks)),
        out_shape=(
            jax.ShapeDtypeStruct(rows.shape, rows.dtype),
            jax.ShapeDtypeStruct((real, node), jnp.float32),
        ),
        in_specs=[SMEM, SMEM] + [VMEM] * (len(blocks) + 4),
        out_specs=(VMEM, VMEM),
        input_output_aliases={2 + len(blocks) + 3: 0},
        compiler_params=PARAMS,
        cost_estimate=cost(1, 4 << 20),
        name="late",
    )(begins, ranked, *blocks, factors, noise, chol, rows)


def tiles(first, count, rows, factors, noise, chol):
    real, node = noise.shape[1:]
    return pl.pallas_call(
        functools.partial(tiles_kernel, first, count),
        out_shape=jax.ShapeDtypeStruct((count, real, node), jnp.float32),
        in_specs=[VMEM] * 4,
        out_specs=VMEM,
        compiler_params=PARAMS,
        cost_estimate=cost(count, 1 << 20),
        name="tiles",
    )(rows, factors, noise, chol)


def exact(a, b):
    return jnp.dot(a, b, precision=lax.Precision.HIGHEST)


def whole(finished, noise, factors, chol, front_w, parents):
    own = finished[:, 0]
    noise, factors, chol = noise[:, 0], factors[:, 0], chol[:, 0]
    count, fan = factors.shape[0], factors.shape[1]
    position = lax.axis_index("sweep")
    small = orders(parents[:, 0], own.shape[0])
    small += tuple((position >= least).astype(jnp.float32) for least in (1, 2, 3, 4, 7))
    mine, theirs, small = spread(own, small)
    begins, ranked, *keep = small

    last_w = front_w[count - 1, 0]
    back1 = from_behind(last_w, 1).astype(jnp.float32)
    back2 = from_behind(last_w, 2).astype(jnp.float32)
    back3 = from_behind(last_w, 3).astype(jnp.float32)
    two = exact(back2, back1)
    three = exact(back3, two)
    six = exact(from_behind(three, 3), three)
    one, two, three, six = keep[1] * back1, keep[2] * two, keep[3] * three, keep[4] * six

    early = mine[: EARLY[0]] + theirs[: EARLY[1]]
    late = mine[EARLY[0] :] + theirs[EARLY[1] :]
    rows, factors, noise, chol, weights = gather_early(
        begins, ranked, early, count * fan, (factors, noise, chol, front_w[:, 0])
    )
    rows, front = gather_late(begins, ranked, late, len(early), factors, noise, chol, rows)
    cut = count // 2
    first = tiles(0, cut, rows, factors, noise, chol)
    second = tiles(cut, count - 1 - cut, rows, factors, noise, chol)
    near = [from_behind(front, by) for by in (1, 2, 3)]
    part = keep[0] * near[0] + exact(near[1], one) + exact(near[2], two)
    incoming = part + exact(from_behind(part, 3), three) + exact(from_behind(part, 6), six)
    local = jnp.concatenate([first, second, front[None]])
    weights = weights.astype(jnp.float32)
    out = local + jnp.einsum("rm,jmn->jrn", incoming, weights, precision=lax.Precision.HIGHEST)
    return out[:, None]


def solution(mesh):
    return jax.shard_map(
        whole,
        mesh=mesh,
        in_specs=(
            P("bench", "sweep", None, None),
            P("bench", "sweep", None, None),
            P("bench", "sweep", None, None, None),
            P("bench", "sweep", None, None),
            P("bench", "sweep", None, None),
            P("bench", "sweep", None),
        ),
        out_specs=P("bench", "sweep", None, None),
        check_vma=False,
    )
```

```python
import functools

import jax
import jax.numpy as jnp
import numpy as np
from jax import lax
from jax.experimental import pallas as pl
from jax.experimental.pallas import tpu as pltpu
from jax.sharding import PartitionSpec as P


SIDE = 4
ORDER = (
    (0, 0, None), (-1, 0, None), (1, 0, None), (0, -1, None), (0, 1, None), (-1, -1, None),
    (-1, 1, None), (1, -1, None), (1, 1, None), (2, 0, None), (0, 2, None), (2, -1, None),
    (2, 1, None), (-1, 2, None), (1, 2, None), (2, 2, 0), (2, 2, 1),
)
BLOCKS = len(ORDER)
EARLY = (13, 11)


def place(x, y, core):
    return ((x % SIDE) * SIDE + y % SIDE) * 2 + core


def offset(core, a, b):
    return (a, b) if core == 0 else (-b, -a)


def fetch(array, a, b):
    pairs = []
    for x in range(SIDE):
        for y in range(SIDE):
            for core in range(2):
                dx, dy = offset(core, a, b)
                pairs.append((place(x + dx, y + dy, core), place(x, y, core)))
    return lax.ppermute(array, "bench", pairs)


def from_partner(array):
    chips = SIDE * SIDE
    pairs = [(2 * i + core, 2 * i + 1 - core) for i in range(chips) for core in range(2)]
    return lax.ppermute(array, "bench", pairs)


def from_behind(array, by):
    size = lax.axis_size("sweep")
    return lax.ppermute(array, "sweep", [(i, (i + by) % size) for i in range(size)])


VIA = {
    (-1, 0, None): ((0, 0, None), (-1, 0)),
    (1, 0, None): ((0, 0, None), (1, 0)),
    (0, -1, None): ((0, 0, None), (0, -1)),
    (0, 1, None): ((0, 0, None), (0, 1)),
    (-1, -1, None): ((-1, 0, None), (0, -1)),
    (-1, 1, None): ((-1, 0, None), (0, 1)),
    (1, -1, None): ((1, 0, None), (0, -1)),
    (1, 1, None): ((1, 0, None), (0, 1)),
    (2, 0, None): ((-1, 0, None), (-1, 0)),
    (0, 2, None): ((0, -1, None), (0, -1)),
    (2, -1, None): ((2, 0, None), (0, -1)),
    (2, 1, None): ((2, 0, None), (0, 1)),
    (-1, 2, None): ((-1, -1, None), (0, -1)),
    (1, 2, None): ((1, 1, None), (0, 1)),
    (2, 2, 0): ((2, -1, None), (0, -1)),
    (2, 2, 1): ((2, 1, None), (0, 1)),
}


def spread(own, small):
    b = {(0, 0, None): own}
    for d, (source, step) in VIA.items():
        block = b[source]
        if d == (0, -1, None):
            own, small = lax.optimization_barrier((own, small))
        if d in ((0, -1, None), (0, 1, None)):
            block = own
        if d[2] is not None:
            block = jnp.split(block, 2)[d[2]]
        b[d] = fetch(block, *step)
    mine = [b[d] for d in ORDER]
    theirs = [from_partner(b[d]) for d in ORDER]
    return mine, theirs, small


def orders(parents, rows):
    number = np.zeros((2, SIDE, SIDE, 2), np.int32)
    for core in range(2):
        for i, (a, b, half) in enumerate(ORDER):
            dx, dy = offset(core, a, b)
            number[core, dx % SIDE, dy % SIDE, slice(None) if half is None else half] = i
    early, late = np.arange(EARLY[0]), np.arange(EARLY[0], BLOCKS)
    theirs_early, theirs_late = np.arange(EARLY[1]), np.arange(EARLY[1], BLOCKS)
    rank = np.zeros((2, BLOCKS), np.int32)
    for i, (other, block) in enumerate(
        [(0, j) for j in early] + [(1, j) for j in theirs_early]
        + [(0, j) for j in late] + [(1, j) for j in theirs_late]
    ):
        rank[other, block] = i
    table = np.zeros((2, 2, 2 * SIDE * SIDE), np.int32)
    for mine in range(2):
        for core in range(2):
            table[mine, core] = rank[int(mine != core)][number[core].reshape(-1)]
    me = lax.axis_index("bench")
    slots = parents.reshape(-1)
    count = slots.shape[0]
    owner = slots // rows
    dx = (owner // (2 * SIDE) - me // (2 * SIDE)) % SIDE
    dy = (owner // 2 - me // 2) % SIDE
    half = (slots % rows) // (rows // 2)
    spot = ((((me % 2) * 2 + owner % 2) * SIDE + dx) * SIDE + dy) * 2 + half
    flat = table.reshape(-1)
    key = jnp.sum(
        jnp.where(spot[None, :] == jnp.arange(flat.size)[:, None], jnp.asarray(flat)[:, None], 0), 0
    )
    slot = jnp.arange(count, dtype=jnp.int32)
    full = key * count + slot
    place_of = jnp.sum((full[:, None] < full[None, :]).astype(jnp.int32), 0)
    packed = slot * rows + slots % rows
    ranked = jnp.sum(jnp.where(place_of[:, None] == slot[None, :], packed[:, None], 0), 0)
    edges = jnp.arange(2 * BLOCKS + 8, dtype=jnp.int32)
    begins = jnp.sum((key[:, None] < edges[None, :]).astype(jnp.int32), 0)
    return begins.astype(jnp.int32), ranked.astype(jnp.int32)


UNROLL = 4


def move_rows(begins, ranked, blocks, first, shift, out):
    for p, block in enumerate(blocks):
        rows = block.shape[0]
        low, high = begins[first + p], begins[first + p + 1]

        def move(i, carry, block=block, low=low, high=high, rows=rows):
            at = [jnp.minimum(low + i * UNROLL + u, high - 1) for u in range(UNROLL)]
            entries = [ranked[j] for j in at]
            values = [block[e & (rows - 1)] for e in entries]
            for e, value in zip(entries, values, strict=True):
                out[e >> shift] = value
            return carry

        lax.fori_loop(0, (high - low + UNROLL - 1) >> 2, move, 0)


def one_tile(t, fan, rows, factors, noise, chol):
    node = factors.shape[-1]
    chosen = jnp.concatenate([rows[t * fan + k] for k in range(fan)], axis=1)
    total = jnp.dot(
        chosen, factors[t].reshape(fan * node, node), preferred_element_type=jnp.float32
    )
    return total + jnp.dot(noise[t], chol[t], preferred_element_type=jnp.float32)


def load_kernel(*refs):
    half, sem = len(refs) // 2, refs[-1]
    copies = [
        pltpu.make_async_copy(source, target, sem.at[i])
        for i, (source, target) in enumerate(zip(refs[:half], refs[half:-1], strict=True))
    ]
    for copy in copies:
        copy.start()
    for copy in copies:
        copy.wait()


def early_kernel(shift, begins, ranked, *refs):
    move_rows(begins, ranked, refs[:-1], 0, shift, refs[-1])


def late_kernel(first, shift, begins, ranked, *refs):
    factors, noise, chol, _, rows, front, local = refs[-7:]
    count, fan = factors.shape[:2]
    move_rows(begins, ranked, refs[:-7], first, shift, rows)
    tile = one_tile(count - 1, fan, rows, factors, noise, chol)
    front[...] = tile
    local[count - 1] = tile


def tiles_kernel(first, count, rows, factors, noise, chol, local_in, local):
    fan = factors.shape[1]
    group = next(g for g in (4, 5, 3, 2, 1) if count % g == 0)

    def step(i, carry):
        at = [first + i * group + u for u in range(group)]
        done = [one_tile(t, fan, rows, factors, noise, chol) for t in at]
        for t, tile in zip(at, done, strict=True):
            local[t] = tile
        return carry

    lax.fori_loop(0, count // group, step, 0)


def final_kernel(steps, incoming, weights, local, out, buffer, sem):
    count, real = local.shape[0], incoming.shape[0]
    high = incoming[...].astype(jnp.bfloat16)
    low = (incoming[...] - high.astype(jnp.float32)).astype(jnp.bfloat16)
    both = jnp.concatenate([high, low], axis=0)
    size = count // steps
    copies = []
    for i in range(steps):
        for t in range(i * size, (i + 1) * size):
            moved = jnp.dot(both, weights[t], preferred_element_type=jnp.float32)
            buffer[t] = local[t] + (moved[:real] + moved[real:])
        span = pl.ds(i * size, size)
        copies.append(pltpu.make_async_copy(buffer.at[span], out.at[span], sem.at[i]))
        copies[-1].start()
    for copy in copies:
        copy.wait()


SMEM = pl.BlockSpec(memory_space=pltpu.SMEM)
VMEM = pl.BlockSpec(memory_space=pltpu.VMEM)
HBM = pl.BlockSpec(memory_space=pltpu.MemorySpace.HBM)
PARAMS = pltpu.CompilerParams(vmem_limit_bytes=8 * 1024 * 1024)


def cost(tiles_count, moved):
    return pl.CostEstimate(
        flops=2 * tiles_count * 64 * 128 * 128 * 9,
        bytes_accessed=moved,
        transcendentals=0,
    )


def shift_of(blocks):
    return max(block.shape[0] for block in blocks).bit_length() - 1


def load(*arrays):
    return pl.pallas_call(
        load_kernel,
        out_shape=[jax.ShapeDtypeStruct(a.shape, a.dtype) for a in arrays],
        in_specs=[HBM] * len(arrays),
        out_specs=[VMEM] * len(arrays),
        scratch_shapes=[pltpu.SemaphoreType.DMA((len(arrays),))],
        compiler_params=PARAMS,
        cost_estimate=cost(0, 16 << 20),
        name="load",
    )(*[pltpu.with_memory_space_constraint(a, pltpu.HBM) for a in arrays])


def gather_early(begins, ranked, blocks, slots):
    shape = (slots,) + blocks[0].shape[1:]
    return pl.pallas_call(
        functools.partial(early_kernel, shift_of(blocks)),
        out_shape=jax.ShapeDtypeStruct(shape, blocks[0].dtype),
        in_specs=[SMEM, SMEM] + [VMEM] * len(blocks),
        out_specs=VMEM,
        compiler_params=PARAMS,
        cost_estimate=cost(0, 4 << 20),
        name="early",
    )(begins, ranked, *blocks)


def gather_late(begins, ranked, blocks, first, factors, noise, chol, rows):
    real, node = noise.shape[1:]
    return pl.pallas_call(
        functools.partial(late_kernel, first, shift_of(blocks)),
        out_shape=(
            jax.ShapeDtypeStruct(rows.shape, rows.dtype),
            jax.ShapeDtypeStruct((real, node), jnp.float32),
            jax.ShapeDtypeStruct((noise.shape[0], real, node), jnp.float32),
        ),
        in_specs=[SMEM, SMEM] + [VMEM] * (len(blocks) + 4),
        out_specs=(VMEM, VMEM, VMEM),
        input_output_aliases={2 + len(blocks) + 3: 0},
        compiler_params=PARAMS,
        cost_estimate=cost(1, 4 << 20),
        name="late",
    )(begins, ranked, *blocks, factors, noise, chol, rows)


def tiles(first, count, rows, factors, noise, chol, local):
    return pl.pallas_call(
        functools.partial(tiles_kernel, first, count),
        out_shape=jax.ShapeDtypeStruct(local.shape, local.dtype),
        in_specs=[VMEM] * 5,
        out_specs=VMEM,
        input_output_aliases={4: 0},
        compiler_params=PARAMS,
        cost_estimate=cost(count, 1 << 20),
        name="tiles",
    )(rows, factors, noise, chol, local)


def finish(incoming, weights, local):
    steps = 8
    return pl.pallas_call(
        functools.partial(final_kernel, steps),
        out_shape=jax.ShapeDtypeStruct(local.shape, local.dtype),
        in_specs=[VMEM] * 3,
        out_specs=HBM,
        scratch_shapes=[
            pltpu.VMEM(local.shape, local.dtype),
            pltpu.SemaphoreType.DMA((steps,)),
        ],
        compiler_params=PARAMS,
        cost_estimate=cost(4, 3 << 20),
        name="finish",
    )(incoming, weights, local)


def exact(a, b):
    return jnp.dot(a, b, precision=lax.Precision.HIGH)


def whole(finished, noise, factors, chol, front_w, parents):
    own = finished[:, 0]
    noise, factors, chol = noise[:, 0], factors[:, 0], chol[:, 0]
    count, fan = factors.shape[0], factors.shape[1]
    position = lax.axis_index("sweep")
    small = orders(parents[:, 0], own.shape[0])
    small += tuple((position >= least).astype(jnp.float32) for least in (1, 2, 3, 4, 7))
    mine, theirs, small = spread(own, small)
    begins, ranked, *keep = small

    last_w = front_w[count - 1, 0]
    back1 = from_behind(last_w, 1).astype(jnp.float32)
    back2 = from_behind(last_w, 2).astype(jnp.float32)
    back3 = from_behind(last_w, 3).astype(jnp.float32)
    two = exact(back2, back1)
    three = exact(back3, two)
    six = exact(from_behind(three, 3), three)
    one, two, three, six = keep[1] * back1, keep[2] * two, keep[3] * three, keep[4] * six

    factors, noise, chol, weights, mine[0] = load(factors, noise, chol, front_w[:, 0], own)
    early = mine[: EARLY[0]] + theirs[: EARLY[1]]
    late = mine[EARLY[0] :] + theirs[EARLY[1] :]
    rows = gather_early(begins, ranked, early, count * fan)
    rows, front, local = gather_late(begins, ranked, late, len(early), factors, noise, chol, rows)
    cut = count // 2
    local = tiles(0, cut, rows, factors, noise, chol, local)
    local = tiles(cut, count - 1 - cut, rows, factors, noise, chol, local)
    near = [from_behind(front, by) for by in (1, 2, 3)]
    part = keep[0] * near[0] + exact(near[1], one) + exact(near[2], two)
    incoming = part + exact(from_behind(part, 3), three) + exact(from_behind(part, 6), six)
    out = finish(incoming, weights, local)
    return out[:, None]


def solution(mesh):
    return jax.shard_map(
        whole,
        mesh=mesh,
        in_specs=(
            P("bench", "sweep", None, None),
            P("bench", "sweep", None, None),
            P("bench", "sweep", None, None, None),
            P("bench", "sweep", None, None),
            P("bench", "sweep", None, None),
            P("bench", "sweep", None),
        ),
        out_specs=P("bench", "sweep", None, None),
        check_vma=False,
    )
```
